256 devices in a mesh: row: 16 (over x, z_lo), col: 16 (over z_hi, y, core).
Axes of the slice: x: 4, y: 4, z: 8 (z_hi: 2, z_lo: 4; z = z_hi * 4 + z_lo), core: 2. Of those that a mesh axis runs over, the one named last changes fastest.
Arguments:
- arriving: float32 [16384, 256], P(('row', 'col')), may hold values from -0.6 to 0.6
- expiring: float32 [16384, 256], P(('row', 'col')), may hold values from -0.6 to 0.6
- taps: float32 [9], replicated, may hold values from -1.4 to 1.4
- covariance: float32 [16384, 16384], P('row', 'col'), may hold values from -1 to 6, as said below
- vectors: float32 [16384, 256], P(('row', 'col')), may hold values from -6 to 6
Outputs:
- updated: float32 [16384, 16384], P('row', 'col')
- basis: float32 [16384, 256], P(('row', 'col'))
The draws below stay inside these ranges and needn't reach their ends.
Inputs may be any that keep to these rules, and one draw needn't show every extreme that they name: `covariance`: symmetric.
All inputs are finite; a program needn't handle non-finite values.
Results may differ from the reference program's by a relative error of at most 0.0013.
Values may be sent and summed in bfloat16 or wider, within the bound.
A program may use at most 128 MiB of HBM per device.

```python
import math
import jax
import jax.numpy as jnp
from jax import lax

CH = 16384
SAMPLES = 256
K = 256
TAPS = 9
HALF = 4


def draw_covariance(key, part):
    noise_key, level_key = jax.random.split(key)
    noise = jnp.clip(jax.random.normal(noise_key, (CH, CH), jnp.float32), -6.0, 6.0)
    coupled = (noise + noise.T) * (0.5 / math.sqrt(2.0 * CH))
    levels = jax.random.uniform(level_key, (CH,), jnp.float32, 2.0, 6.0)
    places = jnp.arange(CH)
    return jnp.where(places[:, None] == places[None, :], levels[:, None], coupled)


def shard_levels(rng, dims, cuts, least, largest):
    factor_of, own = 1.0, jax.random.fold_in(rng, 6)
    for position, blocks in cuts:
        draws = jnp.exp(jax.random.uniform(jax.random.fold_in(own, position), (blocks,), jnp.float32, least / len(cuts), largest / len(cuts)))
        factor_of = factor_of * jnp.repeat(draws, dims[position] // blocks).reshape([-1 if axis == position else 1 for axis in range(len(dims))])
    return factor_of


def gaussian(key, dims, width, bound, shards=(), dtype=jnp.bfloat16):
    level = shard_levels(key, dims, shards, -0.22, 0.18) if shards else 1.0
    result = jax.random.normal(key, dims, jnp.float32) * width * level
    return jnp.minimum(jnp.maximum(result, -bound), bound).astype(dtype)


def setup_inputs(seed: int = 0) -> dict:
    splits = jax.random.split(jax.random.key(seed), 6)
    return {
        "arriving": gaussian(splits[0], (CH, SAMPLES), 0.1, 0.6, ((0, 256),), jnp.float32),
        "expiring": gaussian(splits[1], (CH, SAMPLES), 0.1, 0.6, ((0, 256),), jnp.float32),
        "taps": gaussian(splits[2], (TAPS,), 0.35, 1.4, (), jnp.float32),
        "covariance": draw_covariance(jax.random.fold_in(splits[5], 71), 0),
        "vectors": gaussian(splits[4], (CH, K), 1.0, 6.0, ((0, 256),), jnp.float32),
    }


def spatial_filter(raw, taps):
    padded = jnp.pad(raw, ((HALF, HALF), (0, 0)))
    total = jnp.zeros(raw.shape, jnp.float32)
    for tap in range(TAPS):
        total = total + taps[tap] * padded[tap:tap + CH]
    return total.astype(jnp.bfloat16)

def reference(arriving, expiring, taps, covariance, vectors):
    raw = jnp.concatenate([arriving, expiring], 1)
    filtered = spatial_filter(raw, taps)
    widened = filtered.astype(jnp.float32)
    signed = jnp.concatenate([widened[:, :SAMPLES], -widened[:, SAMPLES:]], 1)
    change = jnp.dot(widened, signed.T, precision=lax.Precision.HIGHEST) / SAMPLES
    updated = covariance + change
    first = jnp.dot(updated, vectors, precision=lax.Precision.HIGHEST)
    second = jnp.dot(updated, first, precision=lax.Precision.HIGHEST)
    gram = jnp.dot(second.T, second, precision=lax.Precision.HIGHEST) / CH
    factor = jnp.linalg.cholesky(gram)
    basis = jax.scipy.linalg.solve_triangular(factor, second.T, lower=True).T
    return (updated, basis)
```

```python
import functools

import jax
import jax.numpy as jnp
from jax import lax
from jax.experimental import pallas as pl
from jax.experimental.pallas import tpu as pltpu
from jax.sharding import PartitionSpec as P

MESH = pl.DeviceIdType.MESH
F32 = jnp.float32
BF16 = jnp.bfloat16
TAPS = 9
NX, NZL, NZH, NY, NC = 4, 4, 2, 4, 2


def split(value):
    high = value.astype(BF16)
    return high, (value - high.astype(F32)).astype(BF16)


def dot(a, b, dims=((1,), (0,))):
    return lax.dot_general(a, b, (dims, ((), ())), preferred_element_type=F32)


def body(
    dims, ch, taps, arr, exp, cov, vec, upd, second_ref, gram_ref,
    raw, covv, cthi, ctlo, uhi, ulo, fr, fc, fsg, vbuf, vhi, vlo, part,
    r1p, r1m, r2p, r2m, red, rz, first, fhi, flo, prod, rc, ry1p, ry1m, ry2p, ry2m,
    ry, rzh, gloc, gc, gh, gy, gs, gzr, gx, gzf, gyf,
    lsem, osem, ssem, rsem,
):
    NX, NZL, NZH, NY, NC = dims
    NB = NZH * NY
    R, C = NX * NZL, NB * NC
    SR = arr.shape[0]
    S = arr.shape[1]
    K = vec.shape[1]
    BLK = SR * R
    r, c = lax.axis_index("row"), lax.axis_index("col")
    x, zl = r // NZL, lax.rem(r, NZL)
    core = lax.rem(c, NC)
    y = lax.rem(c // NC, NY)
    zh = c // (NC * NY)

    def mod(a, n):
        return lax.rem(a + 2 * n, n)

    def rdev(xx, zz):
        return (mod(xx, NX) * NZL + mod(zz, NZL), c)

    def cidx(hh, yy, kk):
        return (mod(hh, NZH) * NY + mod(yy, NY)) * NC + mod(kk, NC)

    def cdev(hh, yy, kk):
        return (r, cidx(hh, yy, kk))

    def rstripe(xx, zz):
        return mod(xx, NX) * NZL + mod(zz, NZL)

    def cpos(hh, yy, kk):
        return mod(kk, NC) * NB + mod(hh, NZH) * NY + mod(yy, NY)

    def rows(ref, index, count):
        return ref.at[pl.ds(pl.multiple_of(index * count, count), count)]

    slots = [0]
    started = []

    def prepare(src, dst, dev):
        k = slots[0]
        slots[0] += 1
        return pltpu.make_async_remote_copy(
            src_ref=src, dst_ref=dst, send_sem=ssem.at[k], recv_sem=rsem.at[k],
            device_id=dev, device_id_type=MESH,
        )

    def send(src, dst, dev):
        copy = prepare(src, dst, dev)
        copy.start()
        started.append(copy)
        return copy

    cov_loads = []
    for k in range(NC):
        for b in range(NB):
            load = pltpu.make_async_copy(
                cov.at[pl.ds((b * NC + k) * SR, SR)],
                covv.at[pl.ds((k * NB + b) * SR, SR)],
                lsem.at[3 + k * NB + b],
            )
            cov_loads.append(load)
    small = [
        pltpu.make_async_copy(arr, raw.at[pl.ds(8, SR), pl.ds(0, S)], lsem.at[0]),
        pltpu.make_async_copy(exp, raw.at[pl.ds(8, SR), pl.ds(S, S)], lsem.at[1]),
        pltpu.make_async_copy(vec, rows(vbuf, cpos(zh, y, core), SR), lsem.at[2]),
    ]
    for load in small + cov_loads:
        load.start()

    barrier = pltpu.get_barrier_semaphore()
    me = r * C + c
    total = R * C
    nxt, prv = lax.rem(me + 1, total), lax.rem(me + total - 1, total)
    next_dev, prev_dev = (nxt // C, lax.rem(nxt, C)), (prv // C, lax.rem(prv, C))
    mirror = (c, r)
    peers = [next_dev, prev_dev]
    peers += [rdev(x + k, zl) for k in range(1, NX)]
    peers += [rdev(x, zl + k) for k in range(1, NZL)]
    peers += [cdev(zh, y + k, core) for k in range(1, NY)]
    peers += [cdev(zh + k, y, core) for k in range(1, NZH)]
    peers += [cdev(zh, y, core + k) for k in range(1, NC)]
    zpeers = []
    for h in range(NZH):
        for k in range(NZL):
            if h > 0 and k > 0:
                zpeers.append((h, k))
    peers += [(rstripe(x, zl + k), cidx(zh + h, y, core)) for h, k in zpeers]
    for peer in peers:
        pl.semaphore_signal(barrier, inc=1, device_id=peer, device_id_type=MESH)

    @pl.when(r != c)
    def _():
        pl.semaphore_signal(barrier, inc=1, device_id=mirror, device_id_type=MESH)

    for load in small + cov_loads:
        load.wait()

    TB = 128

    def flip(i, carry):
        start = pl.multiple_of(i * TB, TB)
        high, low = split(covv[pl.ds(start, TB), :].T)
        cthi[:, pl.ds(start, TB)] = high
        ctlo[:, pl.ds(start, TB)] = low
        return carry

    tiles = BLK // TB
    lax.fori_loop(0, tiles // 2, flip, 0)

    pl.semaphore_wait(barrier, len(peers) + jnp.where(r == c, 0, 1))

    halo_head = send(raw.at[pl.ds(SR, 8)], raw.at[pl.ds(0, 8)], next_dev)
    halo_tail = send(raw.at[pl.ds(8, 8)], raw.at[pl.ds(SR + 8, 8)], prev_dev)

    class ColGather:
        def __init__(self, buf):
            self.buf = buf

        def at(self, h, d, k=0):
            return rows(self.buf, cpos(zh + h, y + d, core + k), SR)

        def push(self, h, d, dev):
            ref = self.at(h, d)
            return send(ref, ref, dev)

        def own(self):
            self.to_zh = [self.push(0, 0, cdev(zh + 1, y, core))] if NZH > 1 else []
            self.up0 = self.push(0, 0, cdev(zh, y + 1, core))
            self.down0 = self.push(0, 0, cdev(zh, y - 1, core))
            self.sib = []
            self.share(0, 0)

        def share(self, h, d):
            if NC > 1:
                self.sib.append(self.push(h, d, cdev(zh, y, core + 1)))

        def near(self):
            self.up0.wait_recv()
            self.relay0 = self.push(0, -1, cdev(zh, y + 1, core))
            self.share(0, -1)
            self.down0.wait_recv()
            self.share(0, 1)

        def far(self):
            if NZH > 1:
                self.to_zh[0].wait_recv()
                self.up1 = self.push(1, 0, cdev(zh, y + 1, core))
                self.down1 = self.push(1, 0, cdev(zh, y - 1, core))
                self.share(1, 0)

        def last(self):
            self.relay0.wait_recv()
            self.share(0, -2)
            if NZH > 1:
                self.down1.wait_recv()
                self.relay1 = self.push(1, 1, cdev(zh, y - 1, core))
                self.share(1, 1)
                self.up1.wait_recv()
                self.share(1, -1)

        def end(self):
            if NZH > 1:
                self.relay1.wait_recv()
                self.share(1, 2)

        def finish(self):
            for copy in self.sib:
                copy.wait_recv()

    class RowGather:
        def __init__(self, buf):
            self.buf = buf

        def push(self, d, k, dev):
            ref = rows(self.buf, rstripe(x + d, zl - k), SR)
            return send(ref, ref, dev)

        def own(self):
            self.line = [self.push(0, 0, rdev(x, zl + k)) for k in range(1, NZL)]
            self.up = [self.push(0, 0, rdev(x + 1, zl))]
            self.down = [self.push(0, 0, rdev(x - 1, zl))]

        def mid(self):
            for k in range(1, NZL):
                self.line[k - 1].wait_recv()
                self.up.append(self.push(0, k, rdev(x + 1, zl)))
                self.down.append(self.push(0, k, rdev(x - 1, zl)))

        def relay(self):
            half = (NZL + 1) // 2
            self.far = []
            for k in range(NZL):
                self.up[k].wait_recv()
                if k < half:
                    self.far.append(self.push(-1, k, rdev(x + 1, zl)))
                self.down[k].wait_recv()
                if k >= half:
                    self.far.append(self.push(1, k, rdev(x - 1, zl)))

        def finish(self):
            for copy in self.far:
                copy.wait_recv()

    vg = ColGather(vbuf)
    vg.own()

    lax.fori_loop(tiles // 2, tiles, flip, 0)

    halo_head.wait_recv()
    halo_tail.wait_recv()
    raw[pl.ds(0, 8), :] = jnp.where(me == 0, 0.0, raw[pl.ds(0, 8), :])
    raw[pl.ds(SR + 8, 8), :] = jnp.where(me == total - 1, 0.0, raw[pl.ds(SR + 8, 8), :])
    acc = jnp.zeros((SR, 2 * S), F32)
    for tap in range(TAPS):
        acc = acc + taps[tap] * raw[pl.ds(4 + tap, SR), :]
    mine = pl.ds(pl.multiple_of(cpos(zh, y, core) * SR, SR), SR)
    fr[mine, :] = acc.astype(BF16)

    cross = prepare(fr.at[mine], rows(fc, c, SR), mirror)
    keep = pltpu.make_async_copy(fr.at[mine], rows(fc, r, SR), lsem.at[0])

    @pl.when(r != c)
    def _():
        cross.start()

    @pl.when(r == c)
    def _():
        keep.start()

    fg = ColGather(fr)
    fg.own()
    vg.near()
    vg.far()
    vg.last()
    vg.end()
    fg.near()

    @pl.when(r != c)
    def _():
        cross.wait_recv()

    @pl.when(r == c)
    def _():
        keep.wait()

    cg = RowGather(fc)
    cg.own()
    fg.far()
    cg.mid()
    fg.last()
    fg.end()
    vg.finish()

    high, low = split(vbuf[...])
    vhi[...] = high
    vlo[...] = low

    SH = BLK // NX

    def start_part(t, carry):
        span = pl.ds(pl.multiple_of(t * SH, SH), SH)
        part[span, :] = (
            dot(cthi[span, :], vhi[...]) + dot(cthi[span, :], vlo[...]) + dot(ctlo[span, :], vhi[...])
        )
        return carry

    cg.relay()
    lax.fori_loop(0, NX, start_part, 0)

    fg.finish()
    mixed = dot(fr[...], vhi[...], ((0,), (0,))) + dot(fr[...], vlo[...], ((0,), (0,)))
    row_id = lax.broadcasted_iota(jnp.int32, mixed.shape, 0)
    mixed = mixed * jnp.where(row_id < S, 1.0 / S, -1.0 / S)
    mhi, mlo = split(mixed)
    cg.finish()

    def add_part(d):
        span = pl.ds(pl.multiple_of(mod(x + d, NX) * SH, SH), SH)
        part[span, :] += dot(fc[span, :], mhi) + dot(fc[span, :], mlo)

    HF = SH // 2

    def half(ref, d, h):
        return ref.at[pl.ds(pl.multiple_of(mod(x + d, NX) * SH + h * HF, HF), HF)]

    xp, xm = rdev(x + 1, zl), rdev(x - 1, zl)
    add_part(2)
    s1p = send(half(part, 2, 0), r1p, xp)
    s1m = send(half(part, 2, 1), r1m, xm)
    add_part(1)
    s2pb = send(half(part, 1, 1), r2p.at[pl.ds(HF, HF)], xp)
    add_part(-1)
    s2ma = send(half(part, -1, 0), r2m.at[pl.ds(0, HF)], xm)
    s1p.wait_recv()
    ref = half(part, 1, 0)
    ref[...] += r1p[...]
    s2pa = send(ref, r2p.at[pl.ds(0, HF)], xp)
    s1m.wait_recv()
    ref = half(part, -1, 1)
    ref[...] += r1m[...]
    s2mb = send(ref, r2m.at[pl.ds(HF, HF)], xm)
    add_part(0)

    col_id = lax.broadcasted_iota(jnp.int32, (1, 2 * S), 1)
    fsg[...] = jnp.where(col_id < S, fr[...], -fr[...])
    UT = min(128, BLK)
    outs = []
    for k in range(NC):
        for b in range(NB):
            outs.append(
                pltpu.make_async_copy(
                    covv.at[pl.ds((k * NB + b) * SR, SR)],
                    upd.at[pl.ds((b * NC + k) * SR, SR)],
                    osem.at[k * NB + b],
                )
            )

    def update(t, carry):
        span = pl.ds(pl.multiple_of(t * UT, UT), UT)
        new = covv[span, :] + dot(fsg[span, :], fc[...], ((1,), (1,))) * (1.0 / S)
        covv[span, :] = new
        high, low = split(new)
        uhi[span, :] = high
        ulo[span, :] = low
        return carry

    lax.fori_loop(0, BLK // UT // 2, update, 0)

    s2pb.wait_recv()
    s2ma.wait_recv()
    s2pa.wait_recv()
    s2mb.wait_recv()
    own_shard = pl.ds(pl.multiple_of(x * SH, SH), SH)
    red[...] = part[own_shard, :] + r2p[...] + r2m[...]
    lines = [
        send(rows(red, mod(zl + k, NZL), SR), rz.at[k - 1], rdev(x, zl + k)) for k in range(1, NZL)
    ]
    lax.fori_loop(BLK // UT // 2, BLK // UT, update, 0)
    for out in outs:
        out.start()
    acc = red[pl.ds(pl.multiple_of(zl * SR, SR), SR), :]
    for k in range(1, NZL):
        lines[k - 1].wait_recv()
        acc = acc + rz[k - 1]
    first[pl.ds(pl.multiple_of(r * SR, SR), SR), :] = acc
    gg = RowGather(first)
    gg.own()
    gg.mid()
    gg.relay()
    gg.finish()

    high, low = split(first[...])
    fhi[...] = high
    flo[...] = low
    HB = NB * SR

    def product(k):
        span = pl.ds(pl.multiple_of(mod(core + k, NC) * HB, HB), HB)
        prod[span, :] = (
            dot(uhi[span, :], fhi[...]) + dot(uhi[span, :], flo[...]) + dot(ulo[span, :], fhi[...])
        )

    if NC > 1:
        product(1)
        to_sib = send(
            prod.at[pl.ds(pl.multiple_of(mod(core + 1, NC) * HB, HB), HB)], rc, cdev(zh, y, core + 1)
        )
    product(0)
    if NC > 1:
        to_sib.wait_recv()
        span = pl.ds(pl.multiple_of(core * HB, HB), HB)
        prod[span, :] += rc[...]

    def piece(h, d):
        return rows(prod, cpos(zh + h, y + d, core), SR)

    yp, ym = cdev(zh, y + 1, core), cdev(zh, y - 1, core)
    hs = list(range(NZH))
    u1 = send(piece(0, 2), ry1p, yp)
    d1 = send(piece(1, 2), ry1m, ym) if NZH > 1 else None
    u2b = send(piece(1, 1), ry2p.at[1], yp) if NZH > 1 else None
    d2a = send(piece(0, -1), ry2m.at[0], ym)
    u1.wait_recv()
    ref = piece(0, 1)
    ref[...] += ry1p[...]
    u2a = send(ref, ry2p.at[0], yp)
    if NZH > 1:
        d1.wait_recv()
        ref = piece(1, -1)
        ref[...] += ry1m[...]
        d2b = send(ref, ry2m.at[1], ym)
        u2b.wait_recv()
        d2b.wait_recv()
        ry[...] = piece(1, 0)[...] + ry2p[1] + ry2m[1]
        cross_zh = send(ry, rzh, cdev(zh + 1, y, core))
    d2a.wait_recv()
    u2a.wait_recv()
    acc = piece(0, 0)[...] + ry2p[0] + ry2m[0]
    if NZH > 1:
        cross_zh.wait_recv()
        acc = acc + rzh[...]
    second_ref[...] = acc

    gloc[...] = lax.dot_general(
        acc, acc, (((0,), (0,)), ((), ())), precision=lax.Precision.HIGHEST, preferred_element_type=F32
    )
    GH = K // NC
    if NC > 1:
        gsib = send(
            gloc.at[pl.ds(pl.multiple_of(mod(core + 1, NC) * GH, GH), GH)], gc, cdev(zh, y, core + 1)
        )
        gsib.wait_recv()
        gh[...] = gloc[pl.ds(pl.multiple_of(core * GH, GH), GH), :] + gc[...]
    else:
        gh[...] = gloc[...]
    GY = GH // NY
    ys = [send(rows(gh, mod(y + k, NY), GY), gy.at[k - 1], cdev(zh, y + k, core)) for k in range(1, NY)]
    acc = gh[pl.ds(pl.multiple_of(y * GY, GY), GY), :]
    for k in range(1, NY):
        ys[k - 1].wait_recv()
        acc = acc + gy[k - 1]
    NT = GY * K // 1024
    LT = K // 128
    for t in range(NT):
        gs[t] = acc[(t // LT) * 8 : (t // LT) * 8 + 8, (t % LT) * 128 : (t % LT) * 128 + 128]
    NZ = NZH * NZL
    TZ = NT // NZ

    def zdev(h, k):
        return (rstripe(x, zl + k), cidx(zh + h, y, core))

    def zid(h, k):
        return mod(zh + h, NZH) * NZL + mod(zl + k, NZL)

    others = [(h, k) for h in range(NZH) for k in range(NZL) if (h, k) != (0, 0)]
    zs = [
        send(rows(gs, zid(h, k), TZ), gzr.at[i], zdev(h, k)) for i, (h, k) in enumerate(others)
    ]
    acc = gs[pl.ds(zid(0, 0) * TZ, TZ)]
    for i in range(len(others)):
        zs[i].wait_recv()
        acc = acc + gzr[i]
    gx[x] = acc
    xs = [send(gx.at[x], gx.at[x], rdev(x + k, zl)) for k in range(1, NX)]
    for copy in xs:
        copy.wait_recv()
    acc = gx[0]
    for k in range(1, NX):
        acc = acc + gx[k]
    mine = zid(0, 0)
    gzf[mine] = acc
    zs = [send(gzf.at[mine], gzf.at[mine], zdev(h, k)) for h, k in others]
    for copy in zs:
        copy.wait_recv()
    for z in range(NZ):
        for t in range(TZ):
            gyf[core, y, z * TZ + t] = gzf[z, t]
    here = gyf.at[core, y]
    ys = [send(here, here, cdev(zh, y + k, core)) for k in range(1, NY)]
    sibs = [send(here, here, cdev(zh, y, core + 1))] if NC > 1 else []
    for k in range(1, NY):
        ys[k - 1].wait_recv()
        if NC > 1:
            ref = gyf.at[core, mod(y - k, NY)]
            sibs.append(send(ref, ref, cdev(zh, y, core + 1)))
    for copy in sibs:
        copy.wait_recv()
    for k in range(NC):
        for j in range(NY):
            for t in range(NT):
                base = k * GH + j * GY + (t // LT) * 8
                gram_ref[base : base + 8, (t % LT) * 128 : (t % LT) * 128 + 128] = gyf[k, j, t] * (1.0 / ch)

    for copy in started:
        copy.wait_send()

    @pl.when(r != c)
    def _():
        cross.wait_send()

    for out in outs:
        out.wait()


def exchange(dims, ch, arriving, expiring, taps, covariance, vectors):
    NX, NZL, NZH, NY, NC = dims
    sr, s = arriving.shape
    k = vectors.shape[1]
    blk = covariance.shape[0]
    sh = blk // NX
    nb = NZH * NY
    gh = k // NC
    gy = gh // NY
    nt = gy * k // 1024
    nz = NZH * NZL
    tz = nt // nz

    def vm(shape, dtype=F32):
        return pltpu.VMEM(shape, dtype)

    scratch = [
        vm((sr + 16, 2 * s)), vm((blk, blk)), vm((blk, blk), BF16), vm((blk, blk), BF16),
        vm((blk, blk), BF16), vm((blk, blk), BF16),
        vm((blk, 2 * s), BF16), vm((blk, 2 * s), BF16), vm((blk, 2 * s), BF16),
        vm((blk, k)), vm((blk, k), BF16), vm((blk, k), BF16), vm((blk, k)),
        vm((sh // 2, k)), vm((sh // 2, k)), vm((sh, k)), vm((sh, k)), vm((sh, k)),
        vm((max(NZL - 1, 1), sr, k)), vm((blk, k)), vm((blk, k), BF16), vm((blk, k), BF16),
        vm((blk, k)), vm((nb * sr, k)),
        vm((sr, k)), vm((sr, k)), vm((2, sr, k)), vm((2, sr, k)), vm((sr, k)), vm((sr, k)),
        vm((k, k)), vm((gh, k)), vm((gh, k)), vm((NY - 1, gy, k)), vm((nt, 8, 128)),
        vm((max(nz - 1, 1), tz, 8, 128)), vm((NX, tz, 8, 128)), vm((nz, tz, 8, 128)), vm((NC, NY, nt, 8, 128)),
        pltpu.SemaphoreType.DMA((3 + NC * nb,)),
        pltpu.SemaphoreType.DMA((NC * nb,)),
        pltpu.SemaphoreType.DMA((128,)),
        pltpu.SemaphoreType.DMA((128,)),
    ]
    hbm = pl.BlockSpec(memory_space=pl.ANY)
    vmem = pl.BlockSpec(memory_space=pltpu.VMEM)
    return pl.pallas_call(
        functools.partial(body, dims, ch),
        out_shape=(
            jax.ShapeDtypeStruct(covariance.shape, F32),
            jax.ShapeDtypeStruct((sr, k), F32),
            jax.ShapeDtypeStruct((k, k), F32),
        ),
        in_specs=[pl.BlockSpec(memory_space=pltpu.SMEM), hbm, hbm, hbm, hbm],
        out_specs=(hbm, vmem, vmem),
        scratch_shapes=scratch,
        compiler_params=pltpu.CompilerParams(
            collective_id=0, has_side_effects=True, vmem_limit_bytes=60000 * 1024
        ),
        name="exchange",
    )(taps, arriving, expiring, covariance, vectors)


def build(mesh, dims):
    def shards(arriving, expiring, taps, covariance, vectors):
        ch = covariance.shape[0] * mesh.shape["row"]
        updated, second, gram = exchange(dims, ch, arriving, expiring, taps, covariance, vectors)
        factor = jnp.linalg.cholesky(gram)
        basis = jax.scipy.linalg.solve_triangular(factor, second.T, lower=True).T
        return (updated, basis)

    in_specs = (
        P(("row", "col"), None),
        P(("row", "col"), None),
        P(),
        P("row", "col"),
        P(("row", "col"), None),
    )
    out_specs = (P("row", "col"), P(("row", "col"), None))
    return jax.shard_map(shards, mesh=mesh, in_specs=in_specs, out_specs=out_specs, check_vma=False)


def solution(mesh):
    return build(mesh, (NX, NZL, NZH, NY, NC))
```

```python
import functools

import jax
import jax.numpy as jnp
from jax import lax
from jax.experimental import pallas as pl
from jax.experimental.pallas import tpu as pltpu
from jax.sharding import PartitionSpec as P

MESH = pl.DeviceIdType.MESH
F32 = jnp.float32
BF16 = jnp.bfloat16
TAPS = 9
NX, NZL, NZH, NY, NC = 4, 4, 2, 4, 2


def split(value):
    high = value.astype(BF16)
    return high, (value - high.astype(F32)).astype(BF16)


def dot(a, b, dims=((1,), (0,))):
    return lax.dot_general(a, b, (dims, ((), ())), preferred_element_type=F32)


def body(
    dims, ch, taps, arr, exp, cov, vec, upd, second_ref, gram_ref,
    raw, covv, cthi, ctlo, uhi, ulo, fr, fc, fsg, vbuf, vhi, vlo, part,
    r1p, r1m, r2p, r2m, red, rz, first, fhi, flo, prod, rc, ry1p, ry1m, ry2p, ry2m,
    ry, rzh, gloc, gc, gh, gy, gs, gzr, gx, gzf, gyf,
    lsem, osem, ssem, rsem,
):
    NX, NZL, NZH, NY, NC = dims
    NB = NZH * NY
    R, C = NX * NZL, NB * NC
    SR = arr.shape[0]
    S = arr.shape[1]
    K = vec.shape[1]
    BLK = SR * R
    r, c = lax.axis_index("row"), lax.axis_index("col")
    x, zl = r // NZL, lax.rem(r, NZL)
    core = lax.rem(c, NC)
    y = lax.rem(c // NC, NY)
    zh = c // (NC * NY)

    def mod(a, n):
        return lax.rem(a + 2 * n, n)

    def rdev(xx, zz):
        return (mod(xx, NX) * NZL + mod(zz, NZL), c)

    def cidx(hh, yy, kk):
        return (mod(hh, NZH) * NY + mod(yy, NY)) * NC + mod(kk, NC)

    def cdev(hh, yy, kk):
        return (r, cidx(hh, yy, kk))

    def rstripe(xx, zz):
        return mod(xx, NX) * NZL + mod(zz, NZL)

    def cpos(hh, yy, kk):
        return mod(kk, NC) * NB + mod(hh, NZH) * NY + mod(yy, NY)

    def rows(ref, index, count):
        return ref.at[pl.ds(pl.multiple_of(index * count, count), count)]

    slots = [0]
    started = []

    def prepare(src, dst, dev):
        k = slots[0]
        slots[0] += 1
        return pltpu.make_async_remote_copy(
            src_ref=src, dst_ref=dst, send_sem=ssem.at[k], recv_sem=rsem.at[k],
            device_id=dev, device_id_type=MESH,
        )

    def send(src, dst, dev):
        copy = prepare(src, dst, dev)
        copy.start()
        started.append(copy)
        return copy

    cov_loads = []
    for k in range(NC):
        for b in range(NB):
            load = pltpu.make_async_copy(
                cov.at[pl.ds((b * NC + k) * SR, SR)],
                covv.at[pl.ds((k * NB + b) * SR, SR)],
                lsem.at[3 + k * NB + b],
            )
            cov_loads.append(load)
    small = [
        pltpu.make_async_copy(arr, raw.at[pl.ds(8, SR), pl.ds(0, S)], lsem.at[0]),
        pltpu.make_async_copy(exp, raw.at[pl.ds(8, SR), pl.ds(S, S)], lsem.at[1]),
        pltpu.make_async_copy(vec, rows(vbuf, cpos(zh, y, core), SR), lsem.at[2]),
    ]
    for load in small + cov_loads:
        load.start()

    barrier = pltpu.get_barrier_semaphore()
    me = r * C + c
    total = R * C
    nxt, prv = lax.rem(me + 1, total), lax.rem(me + total - 1, total)
    next_dev, prev_dev = (nxt // C, lax.rem(nxt, C)), (prv // C, lax.rem(prv, C))
    mirror = (c, r)
    peers = [next_dev, prev_dev]
    peers += [rdev(x + k, zl) for k in range(1, NX)]
    peers += [rdev(x, zl + k) for k in range(1, NZL)]
    peers += [cdev(zh, y + k, core) for k in range(1, NY)]
    peers += [cdev(zh + k, y, core) for k in range(1, NZH)]
    peers += [cdev(zh, y, core + k) for k in range(1, NC)]
    zpeers = []
    for h in range(NZH):
        for k in range(NZL):
            if h > 0 and k > 0:
                zpeers.append((h, k))
    peers += [(rstripe(x, zl + k), cidx(zh + h, y, core)) for h, k in zpeers]
    for peer in peers:
        pl.semaphore_signal(barrier, inc=1, device_id=peer, device_id_type=MESH)

    @pl.when(r != c)
    def _():
        pl.semaphore_signal(barrier, inc=1, device_id=mirror, device_id_type=MESH)

    for load in small + cov_loads:
        load.wait()

    TB = 128

    def flip(i, carry):
        start = pl.multiple_of(i * TB, TB)
        high, low = split(covv[pl.ds(start, TB), :].T)
        cthi[:, pl.ds(start, TB)] = high
        ctlo[:, pl.ds(start, TB)] = low
        return carry

    tiles = BLK // TB
    lax.fori_loop(0, tiles // 2, flip, 0)

    pl.semaphore_wait(barrier, len(peers) + jnp.where(r == c, 0, 1))

    halo_head = send(raw.at[pl.ds(SR, 8)], raw.at[pl.ds(0, 8)], next_dev)
    halo_tail = send(raw.at[pl.ds(8, 8)], raw.at[pl.ds(SR + 8, 8)], prev_dev)

    class ColGather:
        def __init__(self, buf):
            self.buf = buf

        def at(self, h, d, k=0):
            return rows(self.buf, cpos(zh + h, y + d, core + k), SR)

        def push(self, h, d, dev):
            ref = self.at(h, d)
            return send(ref, ref, dev)

        def own(self):
            self.to_zh = [self.push(0, 0, cdev(zh + 1, y, core))] if NZH > 1 else []
            self.up0 = self.push(0, 0, cdev(zh, y + 1, core))
            self.down0 = self.push(0, 0, cdev(zh, y - 1, core))
            self.sib = []
            self.share(0, 0)

        def share(self, h, d):
            if NC > 1:
                self.sib.append(self.push(h, d, cdev(zh, y, core + 1)))

        def near(self):
            self.up0.wait_recv()
            self.relay0 = self.push(0, -1, cdev(zh, y + 1, core))
            self.share(0, -1)
            self.down0.wait_recv()
            self.share(0, 1)

        def far(self):
            if NZH > 1:
                self.to_zh[0].wait_recv()
                self.up1 = self.push(1, 0, cdev(zh, y + 1, core))
                self.down1 = self.push(1, 0, cdev(zh, y - 1, core))
                self.share(1, 0)

        def last(self):
            self.relay0.wait_recv()
            self.share(0, -2)
            if NZH > 1:
                self.down1.wait_recv()
                self.relay1 = self.push(1, 1, cdev(zh, y - 1, core))
                self.share(1, 1)
                self.up1.wait_recv()
                self.share(1, -1)

        def end(self):
            if NZH > 1:
                self.relay1.wait_recv()
                self.share(1, 2)

        def finish(self):
            for copy in self.sib:
                copy.wait_recv()

    class RowGather:
        def __init__(self, buf):
            self.buf = buf

        def push(self, d, k, dev):
            ref = rows(self.buf, rstripe(x + d, zl - k), SR)
            return send(ref, ref, dev)

        def own(self):
            self.line = [self.push(0, 0, rdev(x, zl + k)) for k in range(1, NZL)]
            self.up = [self.push(0, 0, rdev(x + 1, zl))]
            self.down = [self.push(0, 0, rdev(x - 1, zl))]

        def mid(self):
            for k in range(1, NZL):
                self.line[k - 1].wait_recv()
                self.up.append(self.push(0, k, rdev(x + 1, zl)))
                self.down.append(self.push(0, k, rdev(x - 1, zl)))

        def relay(self):
            half = (NZL + 1) // 2
            self.far = []
            for k in range(NZL):
                self.up[k].wait_recv()
                if k < half:
                    self.far.append(self.push(-1, k, rdev(x + 1, zl)))
                self.down[k].wait_recv()
                if k >= half:
                    self.far.append(self.push(1, k, rdev(x - 1, zl)))

        def finish(self):
            for copy in self.far:
                copy.wait_recv()

    vg = ColGather(vbuf)
    vg.own()

    lax.fori_loop(tiles // 2, tiles, flip, 0)

    halo_head.wait_recv()
    halo_tail.wait_recv()
    raw[pl.ds(0, 8), :] = jnp.where(me == 0, 0.0, raw[pl.ds(0, 8), :])
    raw[pl.ds(SR + 8, 8), :] = jnp.where(me == total - 1, 0.0, raw[pl.ds(SR + 8, 8), :])
    acc = jnp.zeros((SR, 2 * S), F32)
    for tap in range(TAPS):
        acc = acc + taps[tap] * raw[pl.ds(4 + tap, SR), :]
    mine = pl.ds(pl.multiple_of(cpos(zh, y, core) * SR, SR), SR)
    fr[mine, :] = acc.astype(BF16)

    cross = prepare(fr.at[mine], rows(fc, c, SR), mirror)
    keep = pltpu.make_async_copy(fr.at[mine], rows(fc, r, SR), lsem.at[0])

    @pl.when(r != c)
    def _():
        cross.start()

    @pl.when(r == c)
    def _():
        keep.start()

    fg = ColGather(fr)
    fg.own()
    vg.near()
    vg.far()
    vg.last()
    vg.end()
    fg.near()

    @pl.when(r != c)
    def _():
        cross.wait_recv()

    @pl.when(r == c)
    def _():
        keep.wait()

    cg = RowGather(fc)
    cg.own()
    fg.far()
    cg.mid()
    fg.last()
    fg.end()
    vg.finish()

    high, low = split(vbuf[...])
    vhi[...] = high
    vlo[...] = low

    SH = BLK // NX

    def start_part(t, carry):
        span = pl.ds(pl.multiple_of(t * SH, SH), SH)
        part[span, :] = (
            dot(cthi[span, :], vhi[...]) + dot(cthi[span, :], vlo[...]) + dot(ctlo[span, :], vhi[...])
        )
        return carry

    cg.relay()
    lax.fori_loop(0, NX, start_part, 0)

    fg.finish()
    mixed = dot(fr[...], vhi[...], ((0,), (0,))) + dot(fr[...], vlo[...], ((0,), (0,)))
    row_id = lax.broadcasted_iota(jnp.int32, mixed.shape, 0)
    mixed = mixed * jnp.where(row_id < S, 1.0 / S, -1.0 / S)
    mhi, mlo = split(mixed)
    cg.finish()

    def add_part(d):
        span = pl.ds(pl.multiple_of(mod(x + d, NX) * SH, SH), SH)
        part[span, :] += dot(fc[span, :], mhi) + dot(fc[span, :], mlo)

    HF = SH // 2

    def half(ref, d, h):
        return ref.at[pl.ds(pl.multiple_of(mod(x + d, NX) * SH + h * HF, HF), HF)]

    xp, xm = rdev(x + 1, zl), rdev(x - 1, zl)
    add_part(2)
    s1p = send(half(part, 2, 0), r1p, xp)
    s1m = send(half(part, 2, 1), r1m, xm)
    add_part(1)
    s2pb = send(half(part, 1, 1), r2p.at[pl.ds(HF, HF)], xp)
    add_part(-1)
    s2ma = send(half(part, -1, 0), r2m.at[pl.ds(0, HF)], xm)
    s1p.wait_recv()
    ref = half(part, 1, 0)
    ref[...] += r1p[...]
    s2pa = send(ref, r2p.at[pl.ds(0, HF)], xp)
    s1m.wait_recv()
    ref = half(part, -1, 1)
    ref[...] += r1m[...]
    s2mb = send(ref, r2m.at[pl.ds(HF, HF)], xm)
    add_part(0)

    col_id = lax.broadcasted_iota(jnp.int32, (1, 2 * S), 1)
    fsg[...] = jnp.where(col_id < S, fr[...], -fr[...])
    UT = min(128, BLK)
    outs = []
    for k in range(NC):
        for b in range(NB):
            outs.append(
                pltpu.make_async_copy(
                    covv.at[pl.ds((k * NB + b) * SR, SR)],
                    upd.at[pl.ds((b * NC + k) * SR, SR)],
                    osem.at[k * NB + b],
                )
            )

    def update(t, carry):
        span = pl.ds(pl.multiple_of(t * UT, UT), UT)
        new = covv[span, :] + dot(fsg[span, :], fc[...], ((1,), (1,))) * (1.0 / S)
        covv[span, :] = new
        high, low = split(new)
        uhi[span, :] = high
        ulo[span, :] = low
        return carry

    lax.fori_loop(0, BLK // UT // 2, update, 0)

    s2pb.wait_recv()
    s2ma.wait_recv()
    s2pa.wait_recv()
    s2mb.wait_recv()
    own_shard = pl.ds(pl.multiple_of(x * SH, SH), SH)
    red[...] = part[own_shard, :] + r2p[...] + r2m[...]
    lines = [
        send(rows(red, mod(zl + k, NZL), SR), rz.at[k - 1], rdev(x, zl + k)) for k in range(1, NZL)
    ]
    lax.fori_loop(BLK // UT // 2, BLK // UT, update, 0)
    for out in outs:
        out.start()
    acc = red[pl.ds(pl.multiple_of(zl * SR, SR), SR), :]
    for k in range(1, NZL):
        lines[k - 1].wait_recv()
        acc = acc + rz[k - 1]
    first[pl.ds(pl.multiple_of(r * SR, SR), SR), :] = acc
    gg = RowGather(first)
    gg.own()
    gg.mid()
    gg.relay()
    gg.finish()

    high, low = split(first[...])
    fhi[...] = high
    flo[...] = low
    HB = NB * SR

    def product(k):
        span = pl.ds(pl.multiple_of(mod(core + k, NC) * HB, HB), HB)
        prod[span, :] = (
            dot(uhi[span, :], fhi[...]) + dot(uhi[span, :], flo[...]) + dot(ulo[span, :], fhi[...])
        )

    if NC > 1:
        product(1)
        to_sib = send(
            prod.at[pl.ds(pl.multiple_of(mod(core + 1, NC) * HB, HB), HB)], rc, cdev(zh, y, core + 1)
        )
    product(0)
    if NC > 1:
        to_sib.wait_recv()
        span = pl.ds(pl.multiple_of(core * HB, HB), HB)
        prod[span, :] += rc[...]

    def piece(h, d):
        return rows(prod, cpos(zh + h, y + d, core), SR)

    yp, ym = cdev(zh, y + 1, core), cdev(zh, y - 1, core)
    hs = list(range(NZH))
    u1 = send(piece(0, 2), ry1p, yp)
    d1 = send(piece(1, 2), ry1m, ym) if NZH > 1 else None
    u2b = send(piece(1, 1), ry2p.at[1], yp) if NZH > 1 else None
    d2a = send(piece(0, -1), ry2m.at[0], ym)
    u1.wait_recv()
    ref = piece(0, 1)
    ref[...] += ry1p[...]
    u2a = send(ref, ry2p.at[0], yp)
    if NZH > 1:
        d1.wait_recv()
        ref = piece(1, -1)
        ref[...] += ry1m[...]
        d2b = send(ref, ry2m.at[1], ym)
        u2b.wait_recv()
        d2b.wait_recv()
        ry[...] = piece(1, 0)[...] + ry2p[1] + ry2m[1]
        cross_zh = send(ry, rzh, cdev(zh + 1, y, core))
    d2a.wait_recv()
    u2a.wait_recv()
    acc = piece(0, 0)[...] + ry2p[0] + ry2m[0]
    if NZH > 1:
        cross_zh.wait_recv()
        acc = acc + rzh[...]
    second_ref[...] = acc

    gloc[...] = lax.dot_general(
        acc, acc, (((0,), (0,)), ((), ())), precision=lax.Precision.HIGHEST, preferred_element_type=F32
    )
    GH = K // NC
    if NC > 1:
        gsib = send(
            gloc.at[pl.ds(pl.multiple_of(mod(core + 1, NC) * GH, GH), GH)], gc, cdev(zh, y, core + 1)
        )
        gsib.wait_recv()
        gh[...] = gloc[pl.ds(pl.multiple_of(core * GH, GH), GH), :] + gc[...]
    else:
        gh[...] = gloc[...]
    GY = GH // NY
    ys = [send(rows(gh, mod(y + k, NY), GY), gy.at[k - 1], cdev(zh, y + k, core)) for k in range(1, NY)]
    acc = gh[pl.ds(pl.multiple_of(y * GY, GY), GY), :]
    for k in range(1, NY):
        ys[k - 1].wait_recv()
        acc = acc + gy[k - 1]
    NT = GY * K // 1024
    LT = K // 128
    for t in range(NT):
        gs[t] = acc[(t // LT) * 8 : (t // LT) * 8 + 8, (t % LT) * 128 : (t % LT) * 128 + 128]
    NZ = NZH * NZL
    TZ = NT // NZ

    def zdev(h, k):
        return (rstripe(x, zl + k), cidx(zh + h, y, core))

    def zid(h, k):
        return mod(zh + h, NZH) * NZL + mod(zl + k, NZL)

    others = [(h, k) for h in range(NZH) for k in range(NZL) if (h, k) != (0, 0)]
    zs = [
        send(rows(gs, zid(h, k), TZ), gzr.at[i], zdev(h, k)) for i, (h, k) in enumerate(others)
    ]
    acc = gs[pl.ds(zid(0, 0) * TZ, TZ)]
    for i in range(len(others)):
        zs[i].wait_recv()
        acc = acc + gzr[i]
    gx[x] = acc
    xs = [send(gx.at[x], gx.at[x], rdev(x + k, zl)) for k in range(1, NX)]
    for copy in xs:
        copy.wait_recv()
    acc = gx[0]
    for k in range(1, NX):
        acc = acc + gx[k]
    mine = zid(0, 0)
    gzf[mine] = acc
    zs = [send(gzf.at[mine], gzf.at[mine], zdev(h, k)) for h, k in others]
    for copy in zs:
        copy.wait_recv()
    for z in range(NZ):
        for t in range(TZ):
            gyf[core, y, z * TZ + t] = gzf[z, t]
    here = gyf.at[core, y]
    ys = [send(here, here, cdev(zh, y + k, core)) for k in range(1, NY)]
    sibs = [send(here, here, cdev(zh, y, core + 1))] if NC > 1 else []
    for k in range(1, NY):
        ys[k - 1].wait_recv()
        if NC > 1:
            ref = gyf.at[core, mod(y - k, NY)]
            sibs.append(send(ref, ref, cdev(zh, y, core + 1)))
    for copy in sibs:
        copy.wait_recv()
    for k in range(NC):
        for j in range(NY):
            for t in range(NT):
                base = k * GH + j * GY + (t // LT) * 8
                gram_ref[base : base + 8, (t % LT) * 128 : (t % LT) * 128 + 128] = gyf[k, j, t] * (1.0 / ch)

    for copy in started:
        copy.wait_send()

    @pl.when(r != c)
    def _():
        cross.wait_send()

    for out in outs:
        out.wait()


STEP = 32


def finish_body(gram, second, upd, basis, out, work, solved, hold, isem, osem):
    n = gram.shape[0]
    m = second.shape[0]
    load = pltpu.make_async_copy(upd, hold, isem)
    load.start()
    work[:, 0:n] = gram[...]
    work[:, n:] = jnp.concatenate([second[...], jnp.zeros((128 - m, n), F32)], 0).T
    wide = n + 128
    store = pltpu.make_async_copy(hold, out, osem)

    def block(k, carry):
        base = pl.multiple_of(k * STEP, STEP)
        rows = work[pl.ds(base, STEP), :]
        lane = pl.multiple_of((k * STEP) // 128 * 128, 128)
        diag = pltpu.roll(
            work[pl.ds(base, STEP), pl.ds(lane, 128)], lax.rem(128 - lax.rem(k * STEP, 128), 128), 1
        )
        full = jnp.concatenate([diag, rows], 1)
        tiles = [full[i * 8 : i * 8 + 8, :] for i in range(STEP // 8)]
        for s in range(STEP // 8):
            cols = [
                [jnp.broadcast_to(tiles[i][:, s * 8 + j : s * 8 + j + 1], (8, 128)) for j in range(8)]
                for i in range(s, STEP // 8)
            ]
            for j in range(8):
                pivot = jnp.broadcast_to(cols[0][j][j : j + 1, :], (8, 128))
                scale = lax.rsqrt(pivot)
                row = tiles[s][j : j + 1, :] * jnp.concatenate([scale[0:1, :]] * (wide // 128 + 1), 1)
                rowb = jnp.broadcast_to(row, (8, wide + 128))
                below = lax.broadcasted_iota(jnp.int32, (8, 128), 0)
                for i in range(s, STEP // 8):
                    factor = cols[i - s][j] * scale
                    if i == s:
                        factor = jnp.where(below > j, factor, 0.0)
                    for q in range(j + 1, 8):
                        entry = jnp.broadcast_to(cols[0][j][q : q + 1, :] * scale[0:1, :], (8, 128))
                        cols[i - s][q] = cols[i - s][q] - factor * entry
                    wide_factor = jnp.concatenate([factor] * (wide // 128 + 1), 1)
                    new = tiles[i] - wide_factor * rowb
                    if i == s:
                        new = jnp.where(
                            lax.broadcasted_iota(jnp.int32, new.shape, 0) == j, rowb, new
                        )
                    tiles[i] = new
        done = jnp.concatenate(tiles, 0)[:, 128:]
        solved[pl.ds(base, STEP), :] = done[:, n:]
        high, low = split(done)
        z = ((0,), (0,))
        hc, lc = high[:, 0:n], low[:, 0:n]
        work[...] -= dot(hc, high, z) + dot(hc, low, z) + dot(lc, high, z)
        return carry

    half = n // STEP // 2
    lax.fori_loop(0, half, block, 0)
    load.wait()
    store.start()
    lax.fori_loop(half, n // STEP, block, 0)
    basis[...] = solved[...].T[0:m, :]
    store.wait()


def finish(gram, second, upd):
    n = gram.shape[0]
    vmem = pl.BlockSpec(memory_space=pltpu.VMEM)
    hbm = pl.BlockSpec(memory_space=pl.ANY)
    return pl.pallas_call(
        finish_body,
        out_shape=(jax.ShapeDtypeStruct(second.shape, F32), jax.ShapeDtypeStruct(upd.shape, F32)),
        in_specs=[vmem, vmem, hbm],
        out_specs=(vmem, hbm),
        scratch_shapes=[
            pltpu.VMEM((n, n + 128), F32), pltpu.VMEM((n, 128), F32), pltpu.VMEM(upd.shape, F32),
            pltpu.SemaphoreType.DMA(()), pltpu.SemaphoreType.DMA(()),
        ],
        compiler_params=pltpu.CompilerParams(vmem_limit_bytes=40000 * 1024),
        name="finish",
    )(gram, second, upd)


def exchange(dims, ch, arriving, expiring, taps, covariance, vectors):
    NX, NZL, NZH, NY, NC = dims
    sr, s = arriving.shape
    k = vectors.shape[1]
    blk = covariance.shape[0]
    sh = blk // NX
    nb = NZH * NY
    gh = k // NC
    gy = gh // NY
    nt = gy * k // 1024
    nz = NZH * NZL
    tz = nt // nz

    def vm(shape, dtype=F32):
        return pltpu.VMEM(shape, dtype)

    scratch = [
        vm((sr + 16, 2 * s)), vm((blk, blk)), vm((blk, blk), BF16), vm((blk, blk), BF16),
        vm((blk, blk), BF16), vm((blk, blk), BF16),
        vm((blk, 2 * s), BF16), vm((blk, 2 * s), BF16), vm((blk, 2 * s), BF16),
        vm((blk, k)), vm((blk, k), BF16), vm((blk, k), BF16), vm((blk, k)),
        vm((sh // 2, k)), vm((sh // 2, k)), vm((sh, k)), vm((sh, k)), vm((sh, k)),
        vm((max(NZL - 1, 1), sr, k)), vm((blk, k)), vm((blk, k), BF16), vm((blk, k), BF16),
        vm((blk, k)), vm((nb * sr, k)),
        vm((sr, k)), vm((sr, k)), vm((2, sr, k)), vm((2, sr, k)), vm((sr, k)), vm((sr, k)),
        vm((k, k)), vm((gh, k)), vm((gh, k)), vm((NY - 1, gy, k)), vm((nt, 8, 128)),
        vm((max(nz - 1, 1), tz, 8, 128)), vm((NX, tz, 8, 128)), vm((nz, tz, 8, 128)), vm((NC, NY, nt, 8, 128)),
        pltpu.SemaphoreType.DMA((3 + NC * nb,)),
        pltpu.SemaphoreType.DMA((NC * nb,)),
        pltpu.SemaphoreType.DMA((128,)),
        pltpu.SemaphoreType.DMA((128,)),
    ]
    hbm = pl.BlockSpec(memory_space=pl.ANY)
    vmem = pl.BlockSpec(memory_space=pltpu.VMEM)
    return pl.pallas_call(
        functools.partial(body, dims, ch),
        out_shape=(
            jax.ShapeDtypeStruct(covariance.shape, F32),
            jax.ShapeDtypeStruct((sr, k), F32),
            jax.ShapeDtypeStruct((k, k), F32),
        ),
        in_specs=[pl.BlockSpec(memory_space=pltpu.SMEM), hbm, hbm, hbm, hbm],
        out_specs=(hbm, vmem, vmem),
        scratch_shapes=scratch,
        compiler_params=pltpu.CompilerParams(
            collective_id=0, has_side_effects=True, vmem_limit_bytes=60000 * 1024
        ),
        name="exchange",
    )(taps, arriving, expiring, covariance, vectors)


def build(mesh, dims):
    def shards(arriving, expiring, taps, covariance, vectors):
        ch = covariance.shape[0] * mesh.shape["row"]
        updated, second, gram = exchange(dims, ch, arriving, expiring, taps, covariance, vectors)
        basis, updated = finish(gram, second, updated)
        return (updated, basis)

    in_specs = (
        P(("row", "col"), None),
        P(("row", "col"), None),
        P(),
        P("row", "col"),
        P(("row", "col"), None),
    )
    out_specs = (P("row", "col"), P(("row", "col"), None))
    return jax.shard_map(shards, mesh=mesh, in_specs=in_specs, out_specs=out_specs, check_vma=False)


def solution(mesh):
    return build(mesh, (NX, NZL, NZH, NY, NC))
```
